32 devices in a mesh: dp: 16 (over z, y, core), ctx: 2 (over x).
Axes of the slice: x: 2, y: 2, z: 4, core: 2. Of those that a mesh axis runs over, the one named last changes fastest.
Arguments:
- params: float32 [7087104], P(('dp', 'ctx')), as said below
- moment_one: float32 [7087104], P(('dp', 'ctx')), may hold values from -6 to 6
- moment_two: float32 [7087104], P(('dp', 'ctx')), may hold values from 0.2048 to 0.8192
- inputs: float32 [16, 256, 768], P('dp', 'ctx'), may hold values from -6 to 6
- cotangent: float32 [16, 256, 768], P('dp', 'ctx'), may hold values from -6 to 6
- doc_ids: int32 [16, 256], P('dp'), may hold values from 0 to 3, never falling along the last dimension, each value on 1 to 128 neighbouring positions
Outputs:
- output: float32 [16, 256, 768], P('dp', 'ctx')
- d_input: float32 [16, 256, 768], P('dp', 'ctx')
- grads: float32 [7087104], P(('dp', 'ctx'))
- new_params: float32 [7087104], P(('dp', 'ctx'))
- new_moment_one: float32 [7087104], P(('dp', 'ctx'))
- new_moment_two: float32 [7087104], P(('dp', 'ctx'))
The draws below stay inside these ranges and needn't reach their ends.
Inputs may be any that keep to these rules, and one draw needn't show every extreme that they name: `doc_ids`: within a sequence the numbers never fall; each of the 4 documents holds 1 to 128 tokens, and one holds exactly 128. `params`: gains lie near one and biases are of order 0.3; a matrix's entries may be up to some 16 times its fan-in scale.
All inputs are finite; a program needn't handle non-finite values.
Results may differ from the reference program's by a relative error of at most 0.02.
The reference program's roundings to bfloat16 on the way count: a program that leaves them out, or rounds other values in their place, can miss the bound.
Values may be sent and summed in bfloat16 or wider, within the bound.
No kernel may reach another device: no remote copies, remote signals or barrier semaphores. Data moves between devices by JAX's collectives and lax.ppermute only.
A program may use at most 256 MiB of HBM per device.

```python
import math
import jax
import jax.numpy as jnp
import numpy as np
from jax import lax

D = 768
HEADS = 12
HEAD_DIM = 64
FF = 3072
DOCS = 4
STEP = 3
LENGTH = 256
SEQS = 16
TOKENS = 4096
PARAMS = 7087104


def draw_params(key, part):
    streams = jax.random.split(key, 16)

    def sample(number, extent, scale):
        values = jax.random.normal(streams[number], extent, jnp.float32) * scale
        return values
    width_scale = D ** (-0.5)
    out_scale = width_scale * (LENGTH / 8.0) ** 0.5
    w_query = sample(2, (D * D,), width_scale)
    w_key = sample(4, (D * D,), width_scale)
    pieces = [1.0 + sample(0, (D,), 0.15), sample(1, (D,), 0.3), w_query, sample(3, (D,), 0.3), w_key, sample(5, (D * D,), width_scale), sample(6, (D,), 0.3), sample(7, (D * D,), out_scale), sample(8, (D,), 0.3), 1.0 + sample(9, (D,), 0.15), sample(10, (D,), 0.3), sample(11, (D * FF,), width_scale), sample(12, (FF,), 0.3), sample(13, (FF * D,), (2.0 / FF) ** 0.5), sample(14, (D,), 0.3)]
    return jnp.concatenate(pieces)


def block_scale(rng, shape, cuts, least, top_value):
    level, own = 1.0, jax.random.fold_in(rng, 6)
    for dim, blocks in cuts:
        draws = jnp.exp(jax.random.uniform(jax.random.fold_in(own, dim), (blocks,), jnp.float32, least / len(cuts), top_value / len(cuts)))
        level = level * jnp.repeat(draws, shape[dim] // blocks).reshape([-1 if axis == dim else 1 for axis in range(len(shape))])
    return level


def profile(count, total, limit, skew):
    loads = [(1 << 20) // math.isqrt(rank ** skew) + 1 for rank in range(2, count + 1)]
    spare, holding = total - limit - (count - 1), [1] * (count - 1)
    while spare > 0:
        free = [i for i in range(count - 1) if holding[i] < limit]
        pool, left = sum([loads[i] for i in free]), spare
        for i in free:
            more = min(limit - holding[i], max(1, left * loads[i] // pool), spare)
            holding[i] = holding[i] + more
            spare = spare - more
    return np.array([limit] + holding)


def ragged(key, number_of, total, reach, skew):
    if number_of == 2:
        one = jax.random.randint(key, (), max(1, total - reach), min(reach, total - 1) + 1)
        return jnp.stack([one, total - one])
    tallies = jnp.asarray(profile(number_of, total, reach, skew), jnp.int32)
    twos = (number_of - 1) // 2
    donor, taker = tallies[1:1 + 2 * twos:2], tallies[2:2 + 2 * twos:2]
    margin = jnp.minimum(donor - 1, reach - taker)
    passed = jax.random.randint(jax.random.fold_in(key, 1), (twos,), 0, 1 << 20) % (margin + 1)
    tallies = tallies.at[1:1 + 2 * twos:2].set(donor - passed).at[2:2 + 2 * twos:2].set(taker + passed)
    return tallies[jax.random.permutation(jax.random.fold_in(key, 2), number_of)]


def bell_draw(rng, shape, scale, limit, cuts=(), kind=jnp.bfloat16):
    result = jax.random.normal(rng, shape, jnp.float32) * scale
    if len(cuts) > 0:
        result = block_scale(rng, shape, cuts, -0.22, 0.18) * result
    return jnp.clip(result, min=-limit, max=limit).astype(kind)


def setup_inputs(seed: int = 0) -> dict:
    streams_of = jax.random.split(jax.random.key(seed), 7)
    return {
        "params": draw_params(jax.random.fold_in(streams_of[6], 71), 0),
        "moment_one": bell_draw(streams_of[1], (PARAMS,), (0.02 * TOKENS ** 0.5), 6.0, ((0, 32),), jnp.float32),
        "moment_two": jnp.clip(jnp.exp(math.log(0.8192) - 1.3862944 * jax.random.uniform(streams_of[2], (PARAMS,), jnp.float32) ** block_scale(streams_of[2], (PARAMS,), ((0, 32),), -0.2, 0.2)), 0.2048, 0.8192),
        "inputs": bell_draw(streams_of[3], (SEQS, LENGTH, D), 1.0, 6.0, ((0, 16), (1, 2)), jnp.float32),
        "cotangent": bell_draw(streams_of[4], (SEQS, LENGTH, D), 1.0, 6.0, ((0, 16), (1, 2)), jnp.float32),
        "doc_ids": jax.vmap(lambda own: jnp.searchsorted(jnp.cumsum(ragged(own, DOCS, LENGTH, LENGTH // 2, 1)), jnp.arange(LENGTH), side="right"))(jax.random.split(streams_of[5], SEQS)).reshape((SEQS, LENGTH)).astype(jnp.int32),
    }


beta_one = 0.9
beta_two = 0.999
learn_rate = 0.02
decay_rate = 0.1
adam_eps = 1e-08
norm_eps = 1e-05

def unpack(flat, width, hidden_width):
    layouts = [(width,), (width,), (width, width), (width,), (width, width), (width, width), (width,), (width, width), (width,), (width,), (width,), (width, hidden_width), (hidden_width,), (hidden_width, width), (width,)]
    pieces = []
    offset = 0
    for layout in layouts:
        number = math.prod(layout)
        pieces.append(lax.slice_in_dim(flat, offset, offset + number).reshape(layout))
        offset += number
    return pieces

def widen(values):
    return values.astype(jnp.float32)

def matmul(left, right):
    return jnp.dot(left, right, preferred_element_type=jnp.float32)

def normalize(values):
    centered = values - lax.optimization_barrier(jnp.mean(values, -1, keepdims=True))
    factor = lax.rsqrt(lax.optimization_barrier(jnp.mean(centered * centered, -1, keepdims=True)) + norm_eps)
    return (centered * factor, factor)

def norm_back(d_normed, normed, factor):
    return factor * (d_normed - lax.optimization_barrier(jnp.mean(d_normed, -1, keepdims=True)) - normed * lax.optimization_barrier(jnp.mean(d_normed * normed, -1, keepdims=True)))

def head_split(values):
    return widen(values).reshape(values.shape[0], HEADS, HEAD_DIM)

def sequence_pass(weights, x_rows, dy_rows, documents):
    gain_one, shift_one, w_query, b_query, w_key, w_value, b_value, w_out, b_out, gain_two, shift_two, w_up, b_up, w_down, b_down = weights
    rows = x_rows.shape[0]
    scale = HEAD_DIM ** (-0.5)
    normed_one, factor_one = normalize(x_rows)
    act_one = (normed_one * widen(gain_one) + widen(shift_one)).astype(jnp.bfloat16)
    query = ((matmul(act_one, w_query) + widen(b_query)) * scale).astype(jnp.bfloat16)
    key_rows = matmul(act_one, w_key).astype(jnp.bfloat16)
    value_rows = (matmul(act_one, w_value) + widen(b_value)).astype(jnp.bfloat16)
    positions = jnp.arange(rows, dtype=jnp.int32)
    allowed = (documents[:, None] == documents[None, :]) & (positions[None, :] <= positions[:, None])
    scores = jnp.einsum('qhd,khd->hqk', head_split(query), head_split(key_rows))
    scores = jnp.where(allowed[None], scores, -jnp.inf)
    top = lax.optimization_barrier(jnp.max(scores, -1, keepdims=True))
    log_total = top + jnp.log(lax.optimization_barrier(jnp.sum(jnp.exp(scores - top), -1, keepdims=True)))
    probs = jnp.exp(scores - log_total)
    probs_b = probs.astype(jnp.bfloat16)
    attended = jnp.einsum('hqk,khd->qhd', widen(probs_b), head_split(value_rows)).reshape(rows, D).astype(jnp.bfloat16)
    hidden = x_rows + matmul(attended, w_out) + widen(b_out)
    normed_two, factor_two = normalize(hidden)
    act_two = (normed_two * widen(gain_two) + widen(shift_two)).astype(jnp.bfloat16)
    pre = matmul(act_two, w_up) + widen(b_up)
    relu_rows = jnp.maximum(pre, 0.0).astype(jnp.bfloat16)
    output = hidden + matmul(relu_rows, w_down) + widen(b_down)
    cot_b = dy_rows.astype(jnp.bfloat16)
    g_b_down = lax.optimization_barrier(jnp.sum(dy_rows, 0))
    g_w_down = matmul(relu_rows.T, cot_b)
    d_pre = jnp.where(pre > 0, matmul(cot_b, w_down.T), 0.0)
    d_pre_b = d_pre.astype(jnp.bfloat16)
    g_b_up = lax.optimization_barrier(jnp.sum(d_pre, 0))
    g_w_up = matmul(act_two.T, d_pre_b)
    d_act_two = matmul(d_pre_b, w_up.T)
    g_gain_two = lax.optimization_barrier(jnp.sum(d_act_two * normed_two, 0))
    g_shift_two = lax.optimization_barrier(jnp.sum(d_act_two, 0))
    d_hidden = dy_rows + norm_back(d_act_two * widen(gain_two), normed_two, factor_two)
    d_hidden_b = d_hidden.astype(jnp.bfloat16)
    g_b_out = lax.optimization_barrier(jnp.sum(d_hidden, 0))
    g_w_out = matmul(attended.T, d_hidden_b)
    d_attended = matmul(d_hidden_b, w_out.T).astype(jnp.bfloat16)
    d_heads = head_split(d_attended)
    d_probs = jnp.einsum('qhd,khd->hqk', d_heads, head_split(value_rows))
    delta = jnp.einsum('qhd,qhd->hq', d_heads, head_split(attended))
    d_scores = (probs * (d_probs - delta[..., None])).astype(jnp.bfloat16)
    d_query_raw = jnp.einsum('hqk,khd->qhd', widen(d_scores), head_split(key_rows)).reshape(rows, D)
    d_key = jnp.einsum('hqk,qhd->khd', widen(d_scores), head_split(query)).reshape(rows, D)
    d_value = jnp.einsum('hqk,qhd->khd', widen(probs_b), d_heads).reshape(rows, D)
    d_query_pre = d_query_raw * scale
    g_b_query = lax.optimization_barrier(jnp.sum(d_query_pre, 0))
    g_b_value = lax.optimization_barrier(jnp.sum(d_value, 0))
    d_query_b = d_query_pre.astype(jnp.bfloat16)
    d_key_b = d_key.astype(jnp.bfloat16)
    d_value_b = d_value.astype(jnp.bfloat16)
    g_w_query = matmul(act_one.T, d_query_b)
    g_w_key = matmul(act_one.T, d_key_b)
    g_w_value = matmul(act_one.T, d_value_b)
    d_act_one = matmul(d_query_b, w_query.T) + matmul(d_key_b, w_key.T) + matmul(d_value_b, w_value.T)
    g_gain_one = lax.optimization_barrier(jnp.sum(d_act_one * normed_one, 0))
    g_shift_one = lax.optimization_barrier(jnp.sum(d_act_one, 0))
    d_input = d_hidden + norm_back(d_act_one * widen(gain_one), normed_one, factor_one)
    gradients = [g_gain_one, g_shift_one, g_w_query, g_b_query, g_w_key, g_w_value, g_b_value, g_w_out, g_b_out, g_gain_two, g_shift_two, g_w_up, g_b_up, g_w_down, g_b_down]
    flat = jnp.concatenate([item.reshape(-1) for item in gradients])
    return (output, d_input, flat)

def reference(params, moment_one, moment_two, inputs, cotangent, doc_ids):
    weights = unpack(params.astype(jnp.bfloat16), D, FF)

    def one_sequence(total, items):
        x_rows, dy_rows, documents = items
        output, d_input, flat = sequence_pass(weights, x_rows, dy_rows, documents)
        return (total + flat, (output, d_input))
    grads, (outputs, d_inputs) = lax.scan(one_sequence, jnp.zeros((PARAMS,), jnp.float32), (inputs, cotangent, doc_ids))
    new_one = beta_one * moment_one + (1.0 - beta_one) * grads
    new_two = beta_two * moment_two + (1.0 - beta_two) * grads * grads
    one_hat = new_one / (1.0 - beta_one ** STEP)
    two_hat = new_two / (1.0 - beta_two ** STEP)
    new_params = params - learn_rate * (one_hat / (jnp.sqrt(two_hat) + adam_eps) + decay_rate * params)
    return (outputs, d_inputs, grads, new_params, new_one, new_two)
```

```python
import math

import jax
import jax.numpy as jnp
from jax import lax
from jax.experimental import pallas as pl
from jax.experimental.pallas import tpu as pltpu
from jax.sharding import Mesh
from jax.sharding import PartitionSpec as P

HEAD_DIM = 64
STEP = 3
LANES = 128
TILE = 16
BLOCK = LANES * TILE

beta_one = 0.9
beta_two = 0.999
learn_rate = 0.02
decay_rate = 0.1
adam_eps = 1e-08
norm_eps = 1e-05

SLOTS = 4


def layout_rows(width, hidden):
    shapes = [
        ("gain_one", (1, width)),
        ("shift_one", (1, width)),
        ("w_query", (width, width)),
        ("b_query", (1, width)),
        ("w_key", (width, width)),
        ("w_value", (width, width)),
        ("b_value", (1, width)),
        ("w_out", (width, width)),
        ("b_out", (1, width)),
        ("gain_two", (1, width)),
        ("shift_two", (1, width)),
        ("w_up", (width, hidden)),
        ("b_up", (1, hidden)),
        ("w_down", (hidden, width)),
        ("b_down", (1, width)),
    ]
    places = {}
    row = 0
    for name, shape in shapes:
        places[name] = (row, shape)
        row += math.prod(shape) // LANES
    return places


class Windows:
    def __init__(self, total, owners):
        self.owners = owners
        self.size = total // owners
        self.starts = [i * self.size // BLOCK * TILE for i in range(owners)]
        self.rows = max(
            -(-((i + 1) * self.size - s * LANES) // BLOCK) * TILE
            for i, s in enumerate(self.starts)
        )
        self.flat_rows = max(-(-total // BLOCK) * TILE, self.starts[-1] + self.rows)

    def start(self, i):
        return i * self.size // BLOCK * TILE


def widen(values):
    return values.astype(jnp.float32)


def matmul(left, right):
    return jnp.dot(left, right, preferred_element_type=jnp.float32)


def normalize(values):
    centered = values - jnp.mean(values, -1, keepdims=True)
    factor = lax.rsqrt(jnp.mean(centered * centered, -1, keepdims=True) + norm_eps)
    return (centered * factor, factor)


def norm_back(d_normed, normed, factor):
    return factor * (
        d_normed
        - jnp.mean(d_normed, -1, keepdims=True)
        - normed * jnp.mean(d_normed * normed, -1, keepdims=True)
    )


def pair_heads(values):
    count, rows, width = values.shape
    pairs = width // (2 * HEAD_DIM)
    return values.reshape(count, rows, pairs, 2, HEAD_DIM).transpose(2, 0, 3, 1, 4)


def join_heads(values):
    pairs, count, two, rows, size = values.shape
    return values.transpose(1, 3, 0, 2, 4).reshape(count, rows, pairs * two * size)


def score_pair(query, keys, allowed):
    scores = jnp.einsum("sgqd,sgkd->sgqk", query, keys, preferred_element_type=jnp.float32)
    return jnp.where(allowed[:, None], scores, -jnp.inf)


MATRICES = ("w_query", "w_key", "w_value", "w_out", "w_up", "w_down")
VECTORS = (
    "gain_one",
    "shift_one",
    "b_query",
    "b_value",
    "b_out",
    "gain_two",
    "shift_two",
    "b_up",
    "b_down",
)


def read_weights(gathered, places, win):
    def kernel(src, *refs):
        outs = refs[: len(MATRICES) + len(VECTORS)]
        flat, ring, sems = refs[len(outs) :]

        def fetch(i, slot):
            return pltpu.make_async_copy(src.at[i], ring.at[slot], sems.at[slot])

        for i in range(min(SLOTS, win.owners)):
            fetch(i, i).start()

        def place(i, carry):
            slot = lax.rem(i, SLOTS)
            fetch(i, slot).wait()
            base = pl.multiple_of(win.start(i), TILE)
            head = widen(ring[slot, :TILE, :])
            before = flat[pl.ds(base, TILE), :]
            flat[pl.ds(base, TILE), :] = jnp.where(i > 0, before, 0.0) + head
            flat[pl.ds(base + TILE, win.rows - TILE), :] = widen(ring[slot, TILE:, :])

            @pl.when(i + SLOTS < win.owners)
            def _():
                fetch(i + SLOTS, slot).start()

            return carry

        lax.fori_loop(0, win.owners, place, 0)
        for name, out in zip(MATRICES + VECTORS, outs):
            row, (depth, width) = places[name]
            wide = width // LANES
            if depth == 1:
                for c in range(wide):
                    out[:, c * LANES : (c + 1) * LANES] = flat[row + c : row + c + 1, :]
                continue
            step = 256

            def move(k, carry):
                for c in range(wide):
                    part = flat[pl.ds(row + k * (step * wide) + c, step, stride=wide), :]
                    out[pl.ds(pl.multiple_of(k * step, step), step), c * LANES : (c + 1) * LANES] = (
                        part.astype(jnp.bfloat16)
                    )
                return carry

            lax.fori_loop(0, depth // step, move, 0)

    shapes = [jax.ShapeDtypeStruct(places[n][1], jnp.bfloat16) for n in MATRICES]
    shapes += [jax.ShapeDtypeStruct(places[n][1], jnp.float32) for n in VECTORS]
    values = pl.pallas_call(
        kernel,
        out_shape=shapes,
        in_specs=[pl.BlockSpec(memory_space=pl.ANY)],
        out_specs=[pl.BlockSpec(memory_space=pltpu.VMEM)] * len(shapes),
        scratch_shapes=[
            pltpu.VMEM((win.flat_rows, LANES), jnp.float32),
            pltpu.VMEM((SLOTS, win.rows, LANES), jnp.bfloat16),
            pltpu.SemaphoreType.DMA((SLOTS,)),
        ],
        name="read_weights",
    )(gathered)
    return dict(zip(MATRICES + VECTORS, values))


def write_grads(pairs, vectors, places, win):
    names = list(pairs)
    operands = [item for name in names for item in pairs[name]]
    vec_names = list(vectors)
    total = sum(math.prod(shape) // LANES for _, shape in places.values())

    def kernel(*refs):
        mats = refs[: len(operands)]
        vecs = refs[len(operands) : len(operands) + len(vec_names)]
        out, flat, ring, sems = refs[len(operands) + len(vec_names) :]
        for name, vec in zip(vec_names, vecs):
            row, (_, width) = places[name]
            for c in range(width // LANES):
                flat[row + c : row + c + 1, :] = vec[:, c * LANES : (c + 1) * LANES]
        if win.flat_rows > total:
            flat[total:, :] = jnp.zeros((win.flat_rows - total, LANES), jnp.float32)
        for n, name in enumerate(names):
            left, right = mats[2 * n], mats[2 * n + 1]
            row, (depth, width) = places[name]
            wide = width // LANES
            step = 256

            for k in range(depth // step):
                piece = lax.dot_general(
                    left[:, k * step : (k + 1) * step],
                    right[...],
                    (((0,), (0,)), ((), ())),
                    preferred_element_type=jnp.float32,
                )
                for c in range(wide):
                    flat[pl.ds(row + k * (step * wide) + c, step, stride=wide), :] = piece[
                        :, c * LANES : (c + 1) * LANES
                    ]

        def send(i, slot):
            return pltpu.make_async_copy(ring.at[slot], out.at[i], sems.at[slot])

        def pack(i, carry):
            slot = lax.rem(i, SLOTS)

            @pl.when(i >= SLOTS)
            def _():
                send(i - SLOTS, slot).wait()

            base = pl.multiple_of(win.start(i), TILE)
            ring[slot] = flat[pl.ds(base, win.rows), :].astype(jnp.bfloat16)
            send(i, slot).start()
            return carry

        lax.fori_loop(0, win.owners, pack, 0)
        for i in range(max(0, win.owners - SLOTS), win.owners):
            send(i, i % SLOTS).wait()

    return pl.pallas_call(
        kernel,
        out_shape=jax.ShapeDtypeStruct((win.owners, win.rows, LANES), jnp.bfloat16),
        in_specs=[pl.BlockSpec(memory_space=pltpu.VMEM)] * (len(operands) + len(vec_names)),
        out_specs=pl.BlockSpec(memory_space=pl.ANY),
        scratch_shapes=[
            pltpu.VMEM((win.flat_rows, LANES), jnp.float32),
            pltpu.VMEM((SLOTS, win.rows, LANES), jnp.bfloat16),
            pltpu.SemaphoreType.DMA((SLOTS,)),
        ],
        name="write_grads",
    )(*operands, *[vectors[n] for n in vec_names])


def make_body(groups, members):
    owners = groups * members
    both = ("far", "core", "ctx")

    def body(params, moment_one, moment_two, inputs, cotangent, doc_ids):
        width = inputs.shape[2]
        total = params.shape[0] * owners
        hidden_width = (total - 4 * width * width - 8 * width) // (2 * width + 1)
        places = layout_rows(width, hidden_width)
        win = Windows(total, owners)
        me = lax.axis_index(both)
        offset = me * win.size - me * win.size // BLOCK * BLOCK
        window = lax.dynamic_update_slice(
            jnp.zeros((win.rows * LANES,), jnp.bfloat16), params.astype(jnp.bfloat16), (offset,)
        ).reshape(win.rows, LANES)
        gathered = lax.all_gather(window, both, axis=0)
        w = read_weights(gathered, places, win)

        rows = inputs.shape[1]
        length = doc_ids.shape[1]
        first = lax.axis_index("ctx") * rows
        scale = HEAD_DIM ** (-0.5)
        normed_one, factor_one = normalize(inputs)
        act_one = (normed_one * w["gain_one"] + w["shift_one"]).astype(jnp.bfloat16)
        query = ((matmul(act_one, w["w_query"]) + w["b_query"]) * scale).astype(jnp.bfloat16)
        key_rows = matmul(act_one, w["w_key"]).astype(jnp.bfloat16)
        value_rows = (matmul(act_one, w["w_value"]) + w["b_value"]).astype(jnp.bfloat16)
        key_all, value_all = (
            lax.all_gather(key_rows, "ctx", axis=1, tiled=True),
            lax.all_gather(value_rows, "ctx", axis=1, tiled=True),
        )
        local_pos = first + jnp.arange(rows, dtype=jnp.int32)
        whole_pos = jnp.arange(length, dtype=jnp.int32)
        local_docs = lax.dynamic_slice_in_dim(doc_ids, first, rows, 1)
        allowed = (local_docs[:, :, None] == doc_ids[:, None, :]) & (
            whole_pos[None, None, :] <= local_pos[None, :, None]
        )
        query_pairs = pair_heads(query)
        key_pairs = pair_heads(key_all)
        value_pairs = pair_heads(value_all)

        def forward_pair(items):
            q_pair, k_pair, v_pair = items
            scores = score_pair(q_pair, k_pair, allowed)
            top = jnp.max(scores, -1, keepdims=True)
            sums = top + jnp.log(jnp.sum(jnp.exp(scores - top), -1, keepdims=True))
            probs_b = jnp.exp(scores - sums).astype(jnp.bfloat16)
            out = jnp.einsum("sgqk,sgkd->sgqd", probs_b, v_pair, preferred_element_type=jnp.float32)
            return (out.astype(jnp.bfloat16), sums[..., 0])

        attended_pairs, log_total = lax.map(forward_pair, (query_pairs, key_pairs, value_pairs))
        attended = join_heads(attended_pairs)
        hidden = inputs + matmul(attended, w["w_out"]) + w["b_out"]
        normed_two, factor_two = normalize(hidden)
        act_two = (normed_two * w["gain_two"] + w["shift_two"]).astype(jnp.bfloat16)
        pre = matmul(act_two, w["w_up"]) + w["b_up"]
        relu_rows = jnp.maximum(pre, 0.0).astype(jnp.bfloat16)
        output = hidden + matmul(relu_rows, w["w_down"]) + w["b_down"]
        cot_b = cotangent.astype(jnp.bfloat16)
        g_b_down = jnp.sum(cotangent, (0, 1))
        d_pre = jnp.where(pre > 0, matmul(cot_b, w["w_down"].T), 0.0)
        d_pre_b = d_pre.astype(jnp.bfloat16)
        g_b_up = jnp.sum(d_pre, (0, 1))
        d_act_two = matmul(d_pre_b, w["w_up"].T)
        g_gain_two = jnp.sum(d_act_two * normed_two, (0, 1))
        g_shift_two = jnp.sum(d_act_two, (0, 1))
        d_hidden = cotangent + norm_back(d_act_two * w["gain_two"], normed_two, factor_two)
        d_hidden_b = d_hidden.astype(jnp.bfloat16)
        g_b_out = jnp.sum(d_hidden, (0, 1))
        d_attended = matmul(d_hidden_b, w["w_out"].T).astype(jnp.bfloat16)
        d_att_pairs = pair_heads(d_attended)
        delta = jnp.einsum("gsjqd,gsjqd->gsjq", widen(d_att_pairs), widen(attended_pairs))

        def query_side(items):
            q_pair, k_pair, v_pair, sums, dd_pair, dl_pair = items
            probs = jnp.exp(score_pair(q_pair, k_pair, allowed) - sums[..., None])
            probs_b = probs.astype(jnp.bfloat16)
            d_probs = jnp.einsum(
                "sgqd,sgkd->sgqk", dd_pair, v_pair, preferred_element_type=jnp.float32
            )
            d_scores = (probs * (d_probs - dl_pair[..., None])).astype(jnp.bfloat16)
            d_q = jnp.einsum("sgqk,sgkd->sgqd", d_scores, k_pair, preferred_element_type=jnp.float32)
            d_k = jnp.einsum("sgqk,sgqd->sgkd", d_scores, q_pair, preferred_element_type=jnp.float32)
            d_v = jnp.einsum("sgqk,sgqd->sgkd", probs_b, dd_pair, preferred_element_type=jnp.float32)
            return (d_q, d_k, d_v)

        d_q_pairs, d_k_pairs, d_v_pairs = lax.map(
            query_side, (query_pairs, key_pairs, value_pairs, log_total, d_att_pairs, delta)
        )
        d_query_raw = join_heads(d_q_pairs)
        d_key_all = join_heads(d_k_pairs)
        d_value_all = join_heads(d_v_pairs)
        d_key, d_value = (
            lax.psum_scatter(d_key_all, "ctx", scatter_dimension=1, tiled=True),
            lax.psum_scatter(d_value_all, "ctx", scatter_dimension=1, tiled=True),
        )
        d_query_pre = d_query_raw * scale
        g_b_query = jnp.sum(d_query_pre, (0, 1))
        g_b_value = jnp.sum(d_value, (0, 1))
        d_query_b = d_query_pre.astype(jnp.bfloat16)
        d_key_b = d_key.astype(jnp.bfloat16)
        d_value_b = d_value.astype(jnp.bfloat16)
        d_act_one = (
            matmul(d_query_b, w["w_query"].T)
            + matmul(d_key_b, w["w_key"].T)
            + matmul(d_value_b, w["w_value"].T)
        )
        g_gain_one = jnp.sum(d_act_one * normed_one, (0, 1))
        g_shift_one = jnp.sum(d_act_one, (0, 1))
        d_input = d_hidden + norm_back(d_act_one * w["gain_one"], normed_one, factor_one)
        pairs = {
            "w_query": (act_one[0], d_query_b[0]),
            "w_key": (act_one[0], d_key_b[0]),
            "w_value": (act_one[0], d_value_b[0]),
            "w_out": (attended[0], d_hidden_b[0]),
            "w_up": (act_two[0], d_pre_b[0]),
            "w_down": (relu_rows[0], cot_b[0]),
        }
        vectors = {
            "gain_one": g_gain_one,
            "shift_one": g_shift_one,
            "b_query": g_b_query,
            "b_value": g_b_value,
            "b_out": g_b_out,
            "gain_two": g_gain_two,
            "shift_two": g_shift_two,
            "b_up": g_b_up,
            "b_down": g_b_down,
        }
        vectors = {name: value[None] for name, value in vectors.items()}
        sections = write_grads(pairs, vectors, places, win)
        core = lax.axis_index("core")
        sections = sections.reshape(groups // 2, 2, members, win.rows, LANES)
        keep = lax.dynamic_index_in_dim(sections, core, 1, keepdims=False)
        give = lax.dynamic_index_in_dim(sections, 1 - core, 1, keepdims=False)
        got = lax.ppermute(give, "core", [(0, 1), (1, 0)])
        half = (widen(keep) + widen(got)).astype(jnp.bfloat16)
        half = half.reshape(owners // 2, win.rows, LANES)
        summed = lax.psum_scatter(half, ("far", "ctx"), scatter_dimension=0, tiled=True)
        grads = lax.dynamic_slice(widen(summed).reshape(-1), (offset,), (win.size,))
        new_one = beta_one * moment_one + (1.0 - beta_one) * grads
        new_two = beta_two * moment_two + (1.0 - beta_two) * grads * grads
        one_hat = new_one / (1.0 - beta_one**STEP)
        two_hat = new_two / (1.0 - beta_two**STEP)
        new_params = params - learn_rate * (
            one_hat / (jnp.sqrt(two_hat) + adam_eps) + decay_rate * params
        )
        return (output, d_input, grads, new_params, new_one, new_two)

    return body


def solution(mesh):
    groups, members = mesh.shape["dp"], mesh.shape["ctx"]
    split = Mesh(mesh.devices.reshape(groups // 2, 2, members), ("far", "core", "ctx"))
    dp = ("far", "core")
    flat = P(("far", "core", "ctx"))
    return jax.shard_map(
        make_body(groups, members),
        mesh=split,
        in_specs=(flat, flat, flat, P(dp, "ctx", None), P(dp, "ctx", None), P(dp, None)),
        out_specs=(P(dp, "ctx", None), P(dp, "ctx", None), flat, flat, flat, flat),
        check_vma=False,
    )
```

```python
import math

import jax
import jax.numpy as jnp
from jax import lax
from jax.experimental import pallas as pl
from jax.experimental.pallas import tpu as pltpu
from jax.sharding import Mesh
from jax.sharding import PartitionSpec as P

HEAD_DIM = 64
STEP = 3
LANES = 128
TILE = 16
BLOCK = LANES * TILE

beta_one = 0.9
beta_two = 0.999
learn_rate = 0.02
decay_rate = 0.1
adam_eps = 1e-08
norm_eps = 1e-05

SLOTS = 4


def layout_rows(width, hidden):
    shapes = [
        ("gain_one", (1, width)),
        ("shift_one", (1, width)),
        ("w_query", (width, width)),
        ("b_query", (1, width)),
        ("w_key", (width, width)),
        ("w_value", (width, width)),
        ("b_value", (1, width)),
        ("w_out", (width, width)),
        ("b_out", (1, width)),
        ("gain_two", (1, width)),
        ("shift_two", (1, width)),
        ("w_up", (width, hidden)),
        ("b_up", (1, hidden)),
        ("w_down", (hidden, width)),
        ("b_down", (1, width)),
    ]
    places = {}
    row = 0
    for name, shape in shapes:
        places[name] = (row, shape)
        row += math.prod(shape) // LANES
    return places


class Windows:
    def __init__(self, total, owners):
        self.owners = owners
        self.size = total // owners
        self.starts = [i * self.size // BLOCK * TILE for i in range(owners)]
        self.rows = max(
            -(-((i + 1) * self.size - s * LANES) // BLOCK) * TILE
            for i, s in enumerate(self.starts)
        )
        self.flat_rows = max(-(-total // BLOCK) * TILE, self.starts[-1] + self.rows)

    def start(self, i):
        return i * self.size // BLOCK * TILE


def widen(values):
    return values.astype(jnp.float32)


def matmul(left, right):
    return jnp.dot(left, right, preferred_element_type=jnp.float32)


def normalize(values):
    centered = values - jnp.mean(values, -1, keepdims=True)
    factor = lax.rsqrt(jnp.mean(centered * centered, -1, keepdims=True) + norm_eps)
    return (centered * factor, factor)


def norm_back(d_normed, normed, factor):
    return factor * (
        d_normed
        - jnp.mean(d_normed, -1, keepdims=True)
        - normed * jnp.mean(d_normed * normed, -1, keepdims=True)
    )


def pair_heads(values):
    count, rows, width = values.shape
    pairs = width // (2 * HEAD_DIM)
    return values.reshape(count, rows, pairs, 2, HEAD_DIM).transpose(2, 0, 3, 1, 4)


def join_heads(values):
    pairs, count, two, rows, size = values.shape
    return values.transpose(1, 3, 0, 2, 4).reshape(count, rows, pairs * two * size)


def score_pair(query, keys, allowed):
    scores = jnp.einsum("sgqd,sgkd->sgqk", query, keys, preferred_element_type=jnp.float32)
    return jnp.where(allowed[:, None], scores, -jnp.inf)


NAMES = (
    "gain_one",
    "shift_one",
    "w_query",
    "b_query",
    "w_key",
    "w_value",
    "b_value",
    "w_out",
    "b_out",
    "gain_two",
    "shift_two",
    "w_up",
    "b_up",
    "w_down",
    "b_down",
)


def read_weights(sources, starts, names, places, win, first, last):
    spots = []
    for number, source in enumerate(sources):
        if source.ndim == 2:
            spots.append((number, None))
        else:
            spots += [(number, k) for k in range(source.shape[0])]
    whole = win.size * win.owners // LANES
    low = first // TILE * TILE
    span = -(-min(last, whole) // TILE) * TILE + win.rows - low
    inner = win.size // BLOCK * TILE

    def kernel(table, *refs):
        srcs = refs[: len(sources)]
        outs = refs[len(sources) : len(sources) + len(names)]
        flat, ring, sems = refs[len(sources) + len(names) :]

        def fetch(n):
            number, k = spots[n]
            src = srcs[number] if k is None else srcs[number].at[k]
            return pltpu.make_async_copy(src, ring.at[n % SLOTS], sems.at[n % SLOTS])

        for n in range(min(SLOTS, len(spots))):
            fetch(n).start()
        edges = [0] + list(range(inner, win.rows, TILE))

        def clear(n, carry):
            base = pl.multiple_of(table[n] - low, TILE)
            for edge in edges:
                flat[pl.ds(base + edge, TILE), :] = jnp.zeros((TILE, LANES), jnp.float32)
            return carry

        lax.fori_loop(0, len(spots), clear, 0)
        for n in range(len(spots)):
            slot = n % SLOTS
            fetch(n).wait()
            base = pl.multiple_of(table[n] - low, TILE)
            flat[pl.ds(base + TILE, inner - TILE), :] = widen(ring[slot, TILE:inner, :])
            for edge in edges:
                where = pl.ds(base + edge, TILE)
                flat[where, :] = flat[where, :] + widen(ring[slot, edge : edge + TILE, :])
            if n + SLOTS < len(spots):
                fetch(n + SLOTS).start()
        for name, out in zip(names, outs):
            row, (depth, width) = places[name]
            row -= low
            wide = width // LANES
            if depth == 1:
                for c in range(wide):
                    out[:, c * LANES : (c + 1) * LANES] = flat[row + c : row + c + 1, :]
                continue
            step = 256

            def move(k, carry):
                for c in range(wide):
                    part = flat[pl.ds(row + k * (step * wide) + c, step, stride=wide), :]
                    out[pl.ds(pl.multiple_of(k * step, step), step), c * LANES : (c + 1) * LANES] = (
                        part.astype(jnp.bfloat16)
                    )
                return carry

            lax.fori_loop(0, depth // step, move, 0)

    shapes = [
        jax.ShapeDtypeStruct(
            places[name][1], jnp.float32 if places[name][1][0] == 1 else jnp.bfloat16
        )
        for name in names
    ]
    values = pl.pallas_call(
        kernel,
        out_shape=shapes,
        in_specs=[pl.BlockSpec(memory_space=pltpu.SMEM)]
        + [pl.BlockSpec(memory_space=pl.ANY)] * len(sources),
        out_specs=[pl.BlockSpec(memory_space=pltpu.VMEM)] * len(shapes),
        scratch_shapes=[
            pltpu.VMEM((span, LANES), jnp.float32),
            pltpu.VMEM((SLOTS, win.rows, LANES), jnp.bfloat16),
            pltpu.SemaphoreType.DMA((SLOTS,)),
        ],
        name="read_weights",
    )(starts, *sources)
    return dict(zip(names, values))


def write_grads(pairs, vectors, starts, counts, places, win, first, last):
    names = list(pairs)
    operands = [item for name in names for item in pairs[name]]
    vec_names = list(vectors)
    whole = win.size * win.owners // LANES
    low = first // TILE * TILE
    high = min(last, whole)
    span = -(-high // TILE) * TILE + win.rows - low
    spots = [(number, k) for number, count in enumerate(counts) for k in range(count)]

    def kernel(table, *refs):
        mats = refs[: len(operands)]
        vecs = refs[len(operands) : len(operands) + len(vec_names)]
        rest = refs[len(operands) + len(vec_names) :]
        outs = rest[: len(counts)]
        flat, ring, sems = rest[len(counts) :]
        if first > low:
            flat[: first - low, :] = jnp.zeros((first - low, LANES), jnp.float32)
        flat[high - low :, :] = jnp.zeros((span - (high - low), LANES), jnp.float32)
        for name, vec in zip(vec_names, vecs):
            row, (_, width) = places[name]
            row -= low
            for c in range(width // LANES):
                flat[row + c : row + c + 1, :] = vec[:, c * LANES : (c + 1) * LANES]
        for n, name in enumerate(names):
            left, right = mats[2 * n], mats[2 * n + 1]
            row, (depth, width) = places[name]
            row -= low
            wide = width // LANES
            step = 256
            for k in range(depth // step):
                piece = lax.dot_general(
                    left[:, k * step : (k + 1) * step],
                    right[...],
                    (((0,), (0,)), ((), ())),
                    preferred_element_type=jnp.float32,
                )
                for c in range(wide):
                    flat[pl.ds(row + k * (step * wide) + c, step, stride=wide), :] = piece[
                        :, c * LANES : (c + 1) * LANES
                    ]

        def send(n):
            number, k = spots[n]
            return pltpu.make_async_copy(
                ring.at[n % SLOTS], outs[number].at[k], sems.at[n % SLOTS]
            )

        for n in range(len(spots)):
            if n >= SLOTS:
                send(n - SLOTS).wait()
            base = pl.multiple_of(table[n] - low, TILE)
            ring[n % SLOTS] = flat[pl.ds(base, win.rows), :].astype(jnp.bfloat16)
            send(n).start()
        for n in range(max(0, len(spots) - SLOTS), len(spots)):
            send(n).wait()

    return pl.pallas_call(
        kernel,
        out_shape=[
            jax.ShapeDtypeStruct((count, win.rows, LANES), jnp.bfloat16) for count in counts
        ],
        in_specs=[pl.BlockSpec(memory_space=pltpu.SMEM)]
        + [pl.BlockSpec(memory_space=pltpu.VMEM)] * (len(operands) + len(vec_names)),
        out_specs=[pl.BlockSpec(memory_space=pl.ANY)] * len(counts),
        scratch_shapes=[
            pltpu.VMEM((span, LANES), jnp.float32),
            pltpu.VMEM((SLOTS, win.rows, LANES), jnp.bfloat16),
            pltpu.SemaphoreType.DMA((SLOTS,)),
        ],
        name="write_grads",
    )(starts, *operands, *[vectors[n] for n in vec_names])


AXES = ("z", "y", "core", "ctx")


class Square:
    def __init__(self, planes):
        self.planes = planes
        shape = (planes, 2, 2, 2)
        spots = [(z, y, c, x) for z in range(planes) for y in (0, 1) for c in (0, 1) for x in (0, 1)]
        number = {spot: n for n, spot in enumerate(spots)}

        def pairs(move):
            return [(number[s], number[move(*s)]) for s in spots]

        self.to_first = pairs(lambda z, y, c, x: (z, y, c, 1 - x) if c == 0 else (z, 1 - y, c, x))
        self.to_second = pairs(lambda z, y, c, x: (z, 1 - y, c, x) if c == 0 else (z, y, c, 1 - x))
        self.to_core = pairs(lambda z, y, c, x: (z, y, 1 - c, x))
        self.hops = {
            (a, b): [(number[s], number[(b,) + s[1:]]) for s in spots if s[0] == a]
            for a in range(planes)
            for b in (a - 1, a + 1)
            if 0 <= b < planes
        }
        self.z, self.y, self.core, self.x = (lax.axis_index(name) for name in AXES)

    def owners(self, plane, far):
        core = self.core if not far else 1 - self.core
        found = []
        for one in (0, 1):
            for two in (0, 1):
                x = self.x ^ jnp.where(core == 0, one, two)
                y = self.y ^ jnp.where(core == 0, two, one)
                found.append(((plane * 2 + y) * 2 + core) * 2 + x)
        return found

    def gather(self, own, planes):
        found = {}
        for plane in planes:
            here = jnp.where(self.z == plane, own, jnp.zeros_like(own))
            for step in (1, -1):
                moved = own
                for a in range(plane, self.planes - 1 if step > 0 else 0, step):
                    moved = lax.ppermute(moved, AXES, self.hops[(a, a + step)])
                    here = here + moved
            one = lax.ppermute(here, AXES, self.to_first)
            two = lax.ppermute(here, AXES, self.to_second)
            three = lax.ppermute(one, AXES, self.to_second)
            near = [here, two, one, three]
            found[plane] = near + [lax.ppermute(item, AXES, self.to_core) for item in near]
        return found

    def reduce(self, near, give):
        got = lax.ppermute(give, AXES, self.to_core)
        message = (widen(near[2:]) + widen(got[2:])).astype(jnp.bfloat16)
        first = lax.ppermute(message, AXES, self.to_first)
        kept = widen(near[:2]) + widen(got[:2]) + widen(first)
        second = lax.ppermute(kept[1].astype(jnp.bfloat16), AXES, self.to_second)
        return kept[0] + widen(second)

    def along(self, plane, mine):
        arrived = []
        for step, begin in ((1, 0), (-1, self.planes - 1)):
            moved = None
            for a in range(begin, plane, step):
                message = mine if moved is None else mine + widen(moved)
                moved = lax.ppermute(message.astype(jnp.bfloat16), AXES, self.hops[(a, a + step)])
            if moved is not None:
                arrived.append(moved)
        result = jnp.where(self.z == plane, mine, 0.0)
        for item in arrived:
            result = result + widen(item)
        return result


def make_body(planes, members):
    owners = planes * 4 * members

    def body(params, moment_one, moment_two, inputs, cotangent, doc_ids):
        width = inputs.shape[2]
        total = params.shape[0] * owners
        hidden_width = (total - 4 * width * width - 8 * width) // (2 * width + 1)
        places = layout_rows(width, hidden_width)
        win = Windows(total, owners)
        me = lax.axis_index(AXES)
        offset = me * win.size - me * win.size // BLOCK * BLOCK
        small = params.astype(jnp.bfloat16)
        window = lax.dynamic_update_slice(
            jnp.zeros((win.rows * LANES,), jnp.bfloat16), small, (offset,)
        ).reshape(win.rows, LANES)
        whole = total // LANES
        border = places["b_value"][0]
        paired = members == 2 and planes > 1 and border * LANES == 8 * win.size
        if paired:
            square = Square(planes)
            early = NAMES[: NAMES.index("b_value")]
            late = NAMES[NAMES.index("b_value") :]

            def starts_of(first, last):
                found = [
                    owner
                    for plane in range(first, last)
                    for far in (False, True)
                    for owner in square.owners(plane, far)
                ]
                return win.start(jnp.stack(found)).astype(jnp.int32)

            early_starts, late_starts = starts_of(0, 1), starts_of(1, planes)
            bias = widen(jnp.where(me == 8, small[:width], 0)).reshape(1, width)
            bias = lax.psum(bias, AXES)
            found = square.gather(window, range(planes))
            w = read_weights(found[0], early_starts, early, places, win, 0, border)
            w["b_value"] = bias
        else:
            starts = win.start(jnp.arange(owners, dtype=jnp.int32))
            gathered = lax.all_gather(window, AXES, axis=0)
            w = read_weights([gathered], starts, NAMES, places, win, 0, whole)

        rows = inputs.shape[1]
        length = doc_ids.shape[1]
        first = lax.axis_index("ctx") * rows
        scale = HEAD_DIM ** (-0.5)
        normed_one, factor_one = normalize(inputs)
        act_one = (normed_one * w["gain_one"] + w["shift_one"]).astype(jnp.bfloat16)
        query = ((matmul(act_one, w["w_query"]) + w["b_query"]) * scale).astype(jnp.bfloat16)
        key_rows = matmul(act_one, w["w_key"]).astype(jnp.bfloat16)
        value_rows = (matmul(act_one, w["w_value"]) + w["b_value"]).astype(jnp.bfloat16)
        local_pos = first + jnp.arange(rows, dtype=jnp.int32)
        local_docs = lax.dynamic_slice_in_dim(doc_ids, first, rows, 1)
        if members == 2:
            other = jnp.concatenate([key_rows, value_rows], 2)
            other = lax.ppermute(other, "ctx", [(0, 1)])
            key_all = jnp.concatenate([key_rows, other[:, :, :width]], 1)
            value_all = jnp.concatenate([value_rows, other[:, :, width:]], 1)
            away = rows - first
            key_pos = jnp.concatenate([local_pos, away + jnp.arange(rows, dtype=jnp.int32)])
            key_docs = jnp.concatenate(
                [local_docs, lax.dynamic_slice_in_dim(doc_ids, away, rows, 1)], 1
            )
        else:
            key_all, value_all = (
                lax.all_gather(key_rows, "ctx", axis=1, tiled=True),
                lax.all_gather(value_rows, "ctx", axis=1, tiled=True),
            )
            key_pos = jnp.arange(length, dtype=jnp.int32)
            key_docs = doc_ids
        allowed = (local_docs[:, :, None] == key_docs[:, None, :]) & (
            key_pos[None, None, :] <= local_pos[None, :, None]
        )
        query_pairs = pair_heads(query)
        key_pairs = pair_heads(key_all)
        value_pairs = pair_heads(value_all)

        def forward_pair(items):
            q_pair, k_pair, v_pair = items
            scores = score_pair(q_pair, k_pair, allowed)
            top = jnp.max(scores, -1, keepdims=True)
            sums = top + jnp.log(jnp.sum(jnp.exp(scores - top), -1, keepdims=True))
            probs_b = jnp.exp(scores - sums).astype(jnp.bfloat16)
            out = jnp.einsum("sgqk,sgkd->sgqd", probs_b, v_pair, preferred_element_type=jnp.float32)
            return (out.astype(jnp.bfloat16), sums[..., 0], jnp.sum(widen(probs_b), -1))

        attended_pairs, log_total, prob_sums = lax.map(forward_pair, (query_pairs, key_pairs, value_pairs))
        attended = join_heads(attended_pairs)
        if paired:
            sources = [item for plane in range(1, planes) for item in found[plane]]
            w.update(
                read_weights(sources, late_starts, late, places, win, border, whole)
            )
        hidden = inputs + matmul(attended, w["w_out"]) + w["b_out"]
        normed_two, factor_two = normalize(hidden)
        act_two = (normed_two * w["gain_two"] + w["shift_two"]).astype(jnp.bfloat16)
        pre = matmul(act_two, w["w_up"]) + w["b_up"]
        relu_rows = jnp.maximum(pre, 0.0).astype(jnp.bfloat16)
        output = hidden + matmul(relu_rows, w["w_down"]) + w["b_down"]
        cot_b = cotangent.astype(jnp.bfloat16)
        g_b_down = jnp.sum(cotangent, (0, 1))
        d_pre = jnp.where(pre > 0, matmul(cot_b, w["w_down"].T), 0.0)
        d_pre_b = d_pre.astype(jnp.bfloat16)
        g_b_up = jnp.sum(d_pre, (0, 1))
        d_act_two = matmul(d_pre_b, w["w_up"].T)
        g_gain_two = jnp.sum(d_act_two * normed_two, (0, 1))
        g_shift_two = jnp.sum(d_act_two, (0, 1))
        d_hidden = cotangent + norm_back(d_act_two * w["gain_two"], normed_two, factor_two)
        d_hidden_b = d_hidden.astype(jnp.bfloat16)
        g_b_out = jnp.sum(d_hidden, (0, 1))
        d_attended = matmul(d_hidden_b, w["w_out"].T).astype(jnp.bfloat16)
        d_att_pairs = pair_heads(d_attended)
        g_b_value = join_heads(widen(d_att_pairs) * prob_sums[..., None]).sum((0, 1))
        pairs = {
            "w_out": (attended[0], d_hidden_b[0]),
            "w_up": (act_two[0], d_pre_b[0]),
            "w_down": (relu_rows[0], cot_b[0]),
        }
        vectors = {
            "b_value": g_b_value,
            "b_out": g_b_out,
            "gain_two": g_gain_two,
            "shift_two": g_shift_two,
            "b_up": g_b_up,
            "b_down": g_b_down,
        }
        if paired:
            counts = [4, 4] * (planes - 1)
            late_vectors = {name: value[None] for name, value in vectors.items()}
            sent = write_grads(
                pairs, late_vectors, late_starts, counts, places, win, border, whole
            )
            shares = [
                square.along(plane, square.reduce(sent[2 * plane - 2], sent[2 * plane - 1]))
                for plane in range(planes - 1, 0, -1)
            ]
        delta = jnp.einsum("gsjqd,gsjqd->gsjq", widen(d_att_pairs), widen(attended_pairs))

        def query_side(items):
            q_pair, k_pair, v_pair, sums, dd_pair, dl_pair = items
            probs = jnp.exp(score_pair(q_pair, k_pair, allowed) - sums[..., None])
            probs_b = probs.astype(jnp.bfloat16)
            d_probs = jnp.einsum(
                "sgqd,sgkd->sgqk", dd_pair, v_pair, preferred_element_type=jnp.float32
            )
            d_scores = (probs * (d_probs - dl_pair[..., None])).astype(jnp.bfloat16)
            d_q = jnp.einsum("sgqk,sgkd->sgqd", d_scores, k_pair, preferred_element_type=jnp.float32)
            d_k = jnp.einsum("sgqk,sgqd->sgkd", d_scores, q_pair, preferred_element_type=jnp.float32)
            d_v = jnp.einsum("sgqk,sgqd->sgkd", probs_b, dd_pair, preferred_element_type=jnp.float32)
            return (d_q, d_k, d_v)

        d_q_pairs, d_k_pairs, d_v_pairs = lax.map(
            query_side, (query_pairs, key_pairs, value_pairs, log_total, d_att_pairs, delta)
        )
        d_query_raw = join_heads(d_q_pairs)
        d_key_all = join_heads(d_k_pairs)
        d_value_all = join_heads(d_v_pairs)
        if members == 2:
            other = jnp.concatenate([d_key_all[:, rows:], d_value_all[:, rows:]], 2)
            other = lax.ppermute(other, "ctx", [(1, 0)])
            d_key = d_key_all[:, :rows] + other[:, :, :width]
            d_value = d_value_all[:, :rows] + other[:, :, width:]
        else:
            d_key, d_value = (
                lax.psum_scatter(d_key_all, "ctx", scatter_dimension=1, tiled=True),
                lax.psum_scatter(d_value_all, "ctx", scatter_dimension=1, tiled=True),
            )
        d_query_pre = d_query_raw * scale
        g_b_query = jnp.sum(d_query_pre, (0, 1))
        d_query_b = d_query_pre.astype(jnp.bfloat16)
        d_key_b = d_key.astype(jnp.bfloat16)
        d_value_b = d_value.astype(jnp.bfloat16)
        d_act_one = (
            matmul(d_query_b, w["w_query"].T)
            + matmul(d_key_b, w["w_key"].T)
            + matmul(d_value_b, w["w_value"].T)
        )
        g_gain_one = jnp.sum(d_act_one * normed_one, (0, 1))
        g_shift_one = jnp.sum(d_act_one, (0, 1))
        d_input = d_hidden + norm_back(d_act_one * w["gain_one"], normed_one, factor_one)
        first_pairs = {
            "w_query": (act_one[0], d_query_b[0]),
            "w_key": (act_one[0], d_key_b[0]),
            "w_value": (act_one[0], d_value_b[0]),
        }
        first_vectors = {
            "gain_one": g_gain_one,
            "shift_one": g_shift_one,
            "b_query": g_b_query,
        }
        if paired:
            first_vectors = {name: value[None] for name, value in first_vectors.items()}
            near, give = write_grads(
                first_pairs, first_vectors, early_starts, [4, 4], places, win, 0, border
            )
            shares.append(square.along(0, square.reduce(near, give)))
            summed = sum(shares)
        else:
            pairs.update(first_pairs)
            vectors.update(first_vectors)
            vectors = {name: value[None] for name, value in vectors.items()}
            (sections,) = write_grads(
                pairs, vectors, starts, [owners], places, win, 0, whole
            )
            summed = widen(lax.psum_scatter(sections, AXES, scatter_dimension=0))
        grads = lax.dynamic_slice(summed.reshape(-1), (offset,), (win.size,))
        new_one = beta_one * moment_one + (1.0 - beta_one) * grads
        new_two = beta_two * moment_two + (1.0 - beta_two) * grads * grads
        one_hat = new_one / (1.0 - beta_one**STEP)
        two_hat = new_two / (1.0 - beta_two**STEP)
        new_params = params - learn_rate * (
            one_hat / (jnp.sqrt(two_hat) + adam_eps) + decay_rate * params
        )
        return (output, d_input, grads, new_params, new_one, new_two)

    return body


def solution(mesh):
    groups, members = mesh.shape["dp"], mesh.shape["ctx"]
    split = Mesh(mesh.devices.reshape(groups // 4, 2, 2, members), AXES)
    dp = AXES[:3]
    flat = P(AXES)
    return jax.shard_map(
        make_body(groups // 4, members),
        mesh=split,
        in_specs=(flat, flat, flat, P(dp, "ctx", None), P(dp, "ctx", None), P(dp, None)),
        out_specs=(P(dp, "ctx", None), P(dp, "ctx", None), flat, flat, flat, flat),
        check_vma=False,
    )
```
